32 devices in a mesh: groups: 2 (over y), frame: 4 (over z), strip: 2 (over x), slab: 2 (over core).
Axes of the slice: x: 2, y: 2, z: 4, core: 2. Of those that a mesh axis runs over, the one named last changes fastest.
Arguments:
- frames_in: bfloat16 [16, 8, 128, 192], P(('groups', 'frame'), 'strip', 'slab'), parts along dimension 0, may hold values from -6 to 6
- weight_first: bfloat16 [3, 3, 3, 192, 192], replicated, may hold values from -0.078125 to 0.078125
- scale_first: float32 [192], replicated, may hold values from 0.25 to 1.75
- weight_second: bfloat16 [3, 3, 3, 192, 192], replicated, may hold values from -0.078125 to 0.078125
- scale_second: float32 [192], replicated, may hold values from 0.25 to 1.75
Outputs:
- latents_out: bfloat16 [16, 8, 128, 192], P(('groups', 'frame'), 'strip', 'slab'), parts along dimension 0
The draws below stay inside these ranges and needn't reach their ends.
There are 2 independent parts, one for each index of `groups`. The reference program is written for one: setup_inputs(seed, part) draws one part's arguments, and reference() takes and returns one part's arrays. A program takes and returns all parts, laid end to end along the dimension named above; an argument that names none is the same for every part. Nothing has to cross between parts.
All inputs are finite; a program needn't handle non-finite values.
Results may differ from the reference program's by a relative error of at most 0.0051.
Values may be sent and summed in bfloat16 or wider, within the bound.
A program may use at most 64 MiB of HBM per device.

```python
import jax
import jax.numpy as jnp
from jax import lax

C = 192
NF = 8
NH = 8
NW = 128


def block_scale(rng, shape, cuts, smallest, largest):
    level, own = 1.0, jax.random.fold_in(rng, 6)
    for position, shards_of in cuts:
        heights = jnp.exp(jax.random.uniform(jax.random.fold_in(own, position), (shards_of,), jnp.float32, smallest / len(cuts), largest / len(cuts)))
        level = level * jnp.repeat(heights, shape[position] // shards_of).reshape([-1 if axis == position else 1 for axis in range(len(shape))])
    return level


def noise(rng, dims, scale, most, cuts=(), held_as=jnp.bfloat16):
    drawn = jax.random.normal(rng, dims, jnp.float32) * scale
    if len(cuts) > 0:
        drawn = block_scale(rng, dims, cuts, -0.22, 0.18) * drawn
    return jnp.clip(drawn, min=-most, max=most).astype(held_as)


def setup_inputs(seed: int = 0, part: int = 0) -> dict:
    splits = jax.random.split(jax.random.key(seed), 6)
    part_keys = jax.random.split(jax.random.fold_in(splits[5], part), 6)
    frames_in = noise(part_keys[0], (NF, NH, NW, C), 1.0, 6.0, ((0, 4), (1, 2), (2, 2)))
    weight_first = noise(splits[1], (3, 3, 3, C, C), (27 * C) ** -0.5, 0.078125)
    scale_first = jnp.clip(1.0 + 0.15 * jax.random.normal(splits[2], (C,), jnp.float32), 0.25, 1.75)
    weight_second = noise(splits[3], (3, 3, 3, C, C), (27 * C) ** -0.5, 0.078125)
    scale_second = jnp.clip(1.0 + 0.15 * jax.random.normal(splits[4], (C,), jnp.float32), 0.25, 1.75)
    return {"frames_in": frames_in, "weight_first": weight_first, "scale_first": scale_first, "weight_second": weight_second, "scale_second": scale_second}


def tap_rows(block, rows, cols):
    pieces = [block[offset_y:offset_y + rows, offset_x:offset_x + cols] for offset_y in range(3) for offset_x in range(3)]
    return jnp.concatenate(pieces, axis=-1).reshape(rows * cols, -1)

def finish(convolved, scales):
    mean_square = lax.optimization_barrier(jnp.mean(convolved * convolved, axis=-1, keepdims=True))
    normed = convolved * lax.rsqrt(mean_square + 1e-06) * scales
    return jax.nn.silu(normed).astype(jnp.bfloat16)

def conv_layer(features, weight, scales):
    channels = features.shape[-1]
    padded = jnp.pad(features, ((2, 0), (1, 1), (1, 1), (0, 0)))
    flat_weight = weight.reshape(3, 9 * channels, channels)

    def single_frame(frame_index):
        window = lax.dynamic_slice_in_dim(padded, frame_index, 3, 0)
        accumulated = jnp.zeros((NH * NW, channels), jnp.float32)
        for offset_t in range(3):
            accumulated = accumulated + jnp.dot(tap_rows(window[offset_t], NH, NW), flat_weight[offset_t], preferred_element_type=jnp.float32)
        return accumulated
    convolved = lax.map(single_frame, jnp.arange(NF, dtype=jnp.int32))
    return finish(convolved, scales).reshape(features.shape)

def reference(frames_in, weight_first, scale_first, weight_second, scale_second):
    hidden = conv_layer(frames_in, weight_first, scale_first)
    return conv_layer(hidden, weight_second, scale_second)
```

```python
import functools

import jax
import jax.numpy as jnp
from jax import lax
from jax.experimental import pallas as pl
from jax.experimental.pallas import tpu as pltpu
from jax.sharding import PartitionSpec as P

MESH = pl.DeviceIdType.MESH
AXES = ("frame", "strip", "slab")


def exists(position, sizes, offsets):
    checks = []
    for index, size, offset in zip(position, sizes, offsets):
        if abs(offset) >= size:
            return None
        if offset > 0:
            checks.append(index < size - offset)
        elif offset < 0:
            checks.append(index >= -offset)
    return functools.reduce(jnp.logical_and, checks) if checks else True


def guarded(condition, action):
    if condition is None:
        return
    if condition is True:
        action()
    else:
        pl.when(condition)(action)


def pack(block):
    lead, half = 128, block.shape[1] // 2
    rest = block[..., lead:]
    return jnp.concatenate([block[..., :lead], jnp.concatenate([rest[:, :half], rest[:, half:]], axis=-1)], axis=1)


def unpack(packed, width):
    rest, lanes = packed[:, width:], packed.shape[-1] // 2
    rest = jnp.concatenate([rest[..., :lanes], rest[..., lanes:]], axis=1)
    return jnp.concatenate([packed[:, :width], rest], axis=-1)


def kernel(
    sizes,
    x_hbm,
    w1_hbm,
    s1_hbm,
    w2_hbm,
    s2_hbm,
    out_ref,
    x_ref,
    scales,
    weights,
    packs,
    edges,
    mains,
    rows,
    tiles,
    taps,
    acc,
    local_sem,
    weight_sem,
    send_sem,
    recv_sem,
):
    frames, height, width, channels = x_ref.shape
    cells = height * width
    position = tuple(lax.axis_index(axis) for axis in AXES)

    def at(offsets):
        return {axis: index + offset for axis, index, offset in zip(AXES, position, offsets)}

    around = [(dz, ds, db) for dz in (0, 1) for ds in (-1, 0, 1) for db in (-1, 0, 1) if (dz, ds, db) != (0, 0, 0)]

    barrier = pltpu.get_barrier_semaphore()
    for offsets in around:
        back = tuple(-o for o in offsets)
        guarded(
            exists(position, sizes, back),
            lambda back=back: pl.semaphore_signal(barrier, inc=1, device_id=at(back), device_id_type=MESH),
        )

    x_loads = [pltpu.make_async_copy(x_hbm.at[frame], x_ref.at[frame], local_sem.at[frame]) for frame in range(2)]
    for frame in (1, 0):
        x_loads[frame].start()

    loads = []
    for layer, source in enumerate((w1_hbm, w2_hbm)):
        for offset_t in (2, 1, 0):
            copy = pltpu.make_async_copy(source.at[offset_t], weights.at[layer, offset_t], weight_sem.at[layer, offset_t])
            copy.start()
            loads.append(copy)
    loads = {(i // 3, 2 - i % 3): copy for i, copy in enumerate(loads)}
    scale_loads = [pltpu.make_async_copy(ref, scales.at[layer], local_sem.at[2 + layer]) for layer, ref in enumerate((s1_hbm, s2_hbm))]
    for copy in scale_loads:
        copy.start()

    def piece(layer, frame, main, offsets):
        dz, ds, db = offsets
        slot = frame if dz else frames + frame
        if db == 0 and ds == 0:
            src, dst, kind = main, mains.at[layer, slot], 0
        elif db == 0:
            row = height - 1 if ds > 0 else 0
            k = 0 if ds > 0 else 1
            src, dst, kind = main.at[row], rows.at[layer, slot, k], 1 + k
        else:
            side = 0 if db > 0 else 1
            src = edges.at[layer, frame, side]
            dst, kind = tiles.at[layer, slot, 1 - ds, side], 3 + 2 * (1 - ds) + side
        return pltpu.make_async_remote_copy(
            src_ref=src,
            dst_ref=dst,
            send_sem=send_sem.at[layer, slot, kind],
            recv_sem=recv_sem.at[layer, slot, kind],
            device_id=at(offsets),
            device_id_type=MESH,
        )

    def fill_edges(layer, frame, block):
        for side, column in ((0, width - 1), (1, 0)):
            picked = jnp.concatenate([block[r, column : column + 1] for r in range(height)], axis=0)
            edges[layer, frame, side, 0:height] = picked.astype(jnp.bfloat16)

    def send(layer, frame, main):
        order = sorted(around, key=lambda o: (o[0], o[2] == 0, o[1] == 0))
        for offsets in order:
            guarded(exists(position, sizes, offsets), lambda o=offsets: piece(layer, frame, main, o).start())

    def receive(layer, slot, main, which):
        for offsets in around:
            if not which(*offsets):
                continue
            back = tuple(-o for o in offsets)
            guarded(exists(position, sizes, back), lambda o=offsets: piece(layer, slot % frames, main, o).wait_recv())

    def shifts(block, first, last):
        column = lax.broadcasted_iota(jnp.int32, block.shape, 1)
        before = jnp.where(column == 0, first, pltpu.roll(block, 1, 1))
        after = jnp.where(column == width - 1, last, pltpu.roll(block, width - 1, 1))
        return [part.astype(jnp.bfloat16) for part in (before, block, after)]

    def fill_taps(slot, shifted):
        pieces = [shifted[x][y : y + height].reshape(cells, channels) for y in range(3) for x in range(3)]
        taps[slot] = jnp.concatenate(pieces, axis=-1)

    def gather(layer, slot, block_ref):
        block = jnp.concatenate([rows[layer, slot, 0][None], block_ref[...], rows[layer, slot, 1][None]], axis=0)
        block = unpack(block, width).astype(jnp.float32)
        halo = []
        for side in range(2):
            above = tiles[layer, slot, 0, side].astype(jnp.float32)
            level = tiles[layer, slot, 1, side].astype(jnp.float32)
            below = tiles[layer, slot, 2, side].astype(jnp.float32)
            picked = [above[height - 1 : height]] + [level[r : r + 1] for r in range(height)] + [below[0:1]]
            halo.append(jnp.stack(picked, axis=0))
        fill_taps(slot, shifts(block, *halo))

    def gather_level(layer, slot, block_ref):
        block = unpack(block_ref[...], width).astype(jnp.float32)
        halo = []
        for side in range(2):
            level = tiles[layer, slot, 1, side].astype(jnp.float32)
            halo.append(jnp.stack([level[r : r + 1] for r in range(height)], axis=0))
        blank = jnp.zeros((1, width, channels), jnp.bfloat16)
        fill_taps(slot, [jnp.concatenate([blank, part, blank], axis=0) for part in shifts(block, *halo)])

    def edge_taps(layer, slot, k):
        block = unpack(rows[layer, slot, k][None], width).astype(jnp.float32)
        pick = slice(height - 1, height) if k == 0 else slice(0, 1)
        halo = [tiles[layer, slot, 2 * k, side].astype(jnp.float32)[pick][None] for side in range(2)]
        return jnp.concatenate(shifts(block, *halo), axis=-1)[0]

    def add_edges(layer):
        for k, ds in ((0, 1), (1, -1)):

            def correct(k=k):
                late, early = (edge_taps(layer, frames + f, k) for f in (1, 0))
                span = pl.ds(6 * k * channels, 3 * channels)
                line = pl.ds(k * (height - 1) * width, width)
                both = jnp.dot(jnp.concatenate([late, early], axis=0), weights[layer, 2, span], preferred_element_type=jnp.float32)
                acc[1, line] += both[:width] + jnp.dot(early, weights[layer, 1, span], preferred_element_type=jnp.float32)
                acc[0, line] += both[width:]

            guarded(exists(position, sizes, (0, -ds, 0)), correct)

    def dot(layer, slot, offset_t, span=slice(None)):
        return jnp.dot(taps[slot, span], weights[layer, offset_t], preferred_element_type=jnp.float32)

    halves = (slice(0, cells // 2), slice(cells // 2, cells))

    def add(layer, frame, slot, offset_t):
        for span in halves:
            acc[frame, span] += dot(layer, slot, offset_t, span)

    def finish(convolved, layer):
        mean_square = jnp.sum(convolved * convolved, axis=-1, keepdims=True) * (1.0 / channels)
        normed = convolved * lax.rsqrt(mean_square + 1e-06) * scales[layer]
        return (normed / (1.0 + jnp.exp(-normed))).reshape(height, width, channels)

    for frame in (1, 0):
        x_loads[frame].wait()
        packs[0, frame] = pack(x_ref[frame])
        fill_edges(0, frame, x_ref[frame].astype(jnp.float32))

    count = jnp.int32(0)
    for offsets in around:
        condition = exists(position, sizes, offsets)
        if condition is not None:
            count = count + (1 if condition is True else condition.astype(jnp.int32))
    pl.semaphore_wait(barrier, count)

    for frame in (1, 0):
        send(0, frame, packs.at[0, frame])

    def zero(ref, condition):
        def clear():
            ref[...] = jnp.zeros_like(ref)

        if condition is None:
            clear()
        elif condition is not True:
            pl.when(jnp.logical_not(condition))(clear)

    for layer in range(2):
        for slot in range(2 * frames):
            dz = 1 if slot < frames else 0
            if dz:
                zero(mains.at[layer, slot], exists(position, sizes, (-1, 0, 0)))
            for k, ds in ((0, 1), (1, -1)):
                zero(rows.at[layer, slot, k], exists(position, sizes, (-dz, -ds, 0)))
            for k in range(3):
                for side, db in ((0, 1), (1, -1)):
                    zero(tiles.at[layer, slot, k, side], exists(position, sizes, (-dz, k - 1, -db)))
    for copy in scale_loads:
        copy.wait()

    def level_tiles(layer, frame):
        receive(layer, frames + frame, packs.at[layer, frame], lambda z, y, x: (z, y) == (0, 0))

    def level(layer, frame):
        gather_level(layer, frames + frame, packs.at[layer, frame])

    def edge_rows(layer):
        for frame in (1, 0):
            receive(layer, frames + frame, packs.at[layer, frame], lambda z, y, x: z == 0 and y != 0)
        add_edges(layer)

    def got(layer, slot):
        receive(layer, slot, mains.at[layer, slot], lambda z, y, x: z == 1)
        gather(layer, slot, mains.at[layer, slot])

    def emit_hidden(frame, values):
        packs[1, frame] = pack(values).astype(jnp.bfloat16)
        fill_edges(1, frame, values)
        send(1, frame, packs.at[1, frame])

    def emit_output(frame, values):
        out_ref[frame] = values.astype(jnp.bfloat16)

    level_tiles(0, 1)
    level_tiles(0, 0)
    loads[0, 2].wait()
    loads[0, 1].wait()
    level(0, 1)
    level(0, 0)
    acc[1] = dot(0, 3, 2)
    acc[0] = dot(0, 2, 2)
    add(0, 1, 2, 1)
    edge_rows(0)
    got(0, 1)
    loads[0, 0].wait()
    add(0, 1, 1, 0)
    emit_hidden(1, finish(acc[1], 0))
    add(0, 0, 1, 1)
    got(0, 0)
    add(0, 0, 0, 0)
    emit_hidden(0, finish(acc[0], 0))

    for offset_t in (2, 1, 0):
        loads[1, offset_t].wait()
    level_tiles(1, 1)
    level(1, 1)
    for span in halves:
        acc[1, span] = dot(1, 3, 2, span)
    level_tiles(1, 0)
    level(1, 0)
    acc[0] = dot(1, 2, 2)
    acc[1] += dot(1, 2, 1)
    edge_rows(1)
    got(1, 1)
    acc[0] += dot(1, 1, 1)
    acc[1] += dot(1, 1, 0)
    emit_output(1, finish(acc[1], 1))
    got(1, 0)
    add(1, 0, 0, 0)
    emit_output(0, finish(acc[0], 1))

    for layer in range(2):
        for frame in (1, 0):
            for offsets in around:
                guarded(
                    exists(position, sizes, offsets),
                    lambda o=offsets: piece(layer, frame, packs.at[layer, frame], o).wait_send(),
                )


def shards(sizes, frames_in, weight_first, scale_first, weight_second, scale_second):
    frames, height, width, channels = frames_in.shape
    anywhere = pl.BlockSpec(memory_space=pl.ANY)
    lines = width * channels // 128
    flat = (3, 9 * channels, channels)
    half = jnp.bfloat16
    return pl.pallas_call(
        functools.partial(kernel, sizes),
        out_shape=pltpu.VMEM(frames_in.shape, half),
        in_specs=[anywhere] * 5,
        out_specs=pl.BlockSpec(memory_space=pltpu.VMEM),
        scratch_shapes=[
            pltpu.VMEM(frames_in.shape, half),
            pltpu.VMEM((2, 1, channels), jnp.float32),
            pltpu.VMEM((2, *flat), half),
            pltpu.VMEM((2, frames, height, lines, 128), half),
            pltpu.VMEM((2, frames, 2, 8, channels), half),
            pltpu.VMEM((2, frames, height, lines, 128), half),
            pltpu.VMEM((2, 2 * frames, 2, lines, 128), half),
            pltpu.VMEM((2, 2 * frames, 3, 2, 8, channels), half),
            pltpu.VMEM((2 * frames, height * width, 9 * channels), half),
            pltpu.VMEM((frames, height * width, channels), jnp.float32),
            pltpu.SemaphoreType.DMA((4,)),
            pltpu.SemaphoreType.DMA((2, 3)),
            pltpu.SemaphoreType.DMA((2, 2 * frames, 9)),
            pltpu.SemaphoreType.DMA((2, 2 * frames, 9)),
        ],
        compiler_params=pltpu.CompilerParams(collective_id=0, has_side_effects=True),
        name="conv_block",
    )(
        frames_in,
        weight_first.reshape(flat),
        scale_first.reshape(1, channels),
        weight_second.reshape(flat),
        scale_second.reshape(1, channels),
    )


def solution(mesh):
    sizes = tuple(mesh.shape[axis] for axis in AXES)
    return jax.shard_map(
        functools.partial(shards, sizes),
        mesh=mesh,
        in_specs=(P(("groups", "frame"), "strip", "slab", None), P(), P(), P(), P()),
        out_specs=P(("groups", "frame"), "strip", "slab", None),
        check_vma=False,
    )
```

```python
import functools

import jax
import jax.numpy as jnp
from jax import lax
from jax.experimental import pallas as pl
from jax.experimental.pallas import tpu as pltpu
from jax.sharding import PartitionSpec as P

MESH = pl.DeviceIdType.MESH
AXES = ("frame", "strip", "slab")


def exists(position, sizes, offsets):
    checks = []
    for index, size, offset in zip(position, sizes, offsets):
        if abs(offset) >= size:
            return None
        if offset > 0:
            checks.append(index < size - offset)
        elif offset < 0:
            checks.append(index >= -offset)
    return functools.reduce(jnp.logical_and, checks) if checks else True


def guarded(condition, action):
    if condition is None:
        return
    if condition is True:
        action()
    else:
        pl.when(condition)(action)


def ways(sizes):
    return tuple(2 if size > 2 else 1 for size in sizes[1:])


def kind_counts(sizes):
    strips, slabs = ways(sizes)
    late = 1 + slabs + strips + strips * slabs
    return late, 2 * late - 1


def pack(block):
    lead, half = 128, block.shape[1] // 2
    rest = block[..., lead:]
    return jnp.concatenate([block[..., :lead], jnp.concatenate([rest[:, :half], rest[:, half:]], axis=-1)], axis=1)


def unpack(packed, width):
    rest, lanes = packed[:, width:], packed.shape[-1] // 2
    rest = jnp.concatenate([rest[..., :lanes], rest[..., lanes:]], axis=1)
    return jnp.concatenate([packed[:, :width], rest], axis=-1)


def kernel(
    sizes,
    x_hbm,
    w1_hbm,
    s1_hbm,
    w2_hbm,
    s2_hbm,
    out_ref,
    x_ref,
    scales,
    weights,
    packs,
    edges,
    mains,
    rows,
    tiles,
    taps,
    acc,
    local_sem,
    send_sem,
    recv_sem,
    ready,
):
    frames, height, width, channels = x_ref.shape
    cells = height * width
    position = tuple(lax.axis_index(axis) for axis in AXES)

    def at(offsets):
        return {axis: index + offset for axis, index, offset in zip(AXES, position, offsets)}

    around = [(dz, ds, db) for dz in (0, 1) for ds in (-1, 0, 1) for db in (-1, 0, 1) if (dz, ds, db) != (0, 0, 0)]

    near = [offsets for offsets in around if not (offsets[0] and offsets[1])]

    barrier = pltpu.get_barrier_semaphore()
    for offsets in near:
        back = tuple(-o for o in offsets)
        guarded(
            exists(position, sizes, back),
            lambda back=back: pl.semaphore_signal(barrier, inc=1, device_id=at(back), device_id_type=MESH),
        )

    x_loads = [pltpu.make_async_copy(x_hbm.at[frame], x_ref.at[frame], local_sem.at[frame]) for frame in range(frames)]
    for frame in reversed(range(frames)):
        x_loads[frame].start()

    loads = {(0, t): pltpu.make_async_copy(w1_hbm.at[t], weights.at[0, t], local_sem.at[t]) for t in (2, 1, 0)}
    loads[1] = pltpu.make_async_copy(w2_hbm, weights.at[1], local_sem.at[3])
    scale_loads = [pltpu.make_async_copy(ref, scales.at[layer], local_sem.at[4 + layer]) for layer, ref in enumerate((s1_hbm, s2_hbm))]

    strips, slabs = ways(sizes)
    late_kinds, kinds = kind_counts(sizes)

    def piece(layer, frame, main, offsets):
        dz, ds, db = offsets
        slot = frame if dz else frames + frame
        k = 0 if ds > 0 else 1
        side = 0 if db > 0 else 1
        if db == 0 and ds == 0:
            src, dst, kind = main, mains.at[layer, slot], 0
        elif db == 0:
            row = height - 1 if ds > 0 else 0
            src, dst, kind = main.at[row], rows.at[layer, slot, k], 1 + slabs + k % strips
        else:
            src, dst = edges.at[layer, frame, side], tiles.at[layer, slot, 1 - ds, side]
            kind = 1 + side % slabs if ds == 0 else 1 + slabs + strips + (k % strips) * slabs + side % slabs
        index = frame * kinds + (kind if dz else late_kinds + kind - 1)
        return pltpu.make_async_remote_copy(
            src_ref=src,
            dst_ref=dst,
            send_sem=send_sem.at[index],
            recv_sem=recv_sem.at[layer, index],
            device_id=at(offsets),
            device_id_type=MESH,
        )

    def wait_sent(layer, frame):
        for offsets in around:
            guarded(
                exists(position, sizes, offsets),
                lambda o=offsets: piece(layer, frame, packs.at[layer, frame], o).wait_send(),
            )

    def fill_edges(layer, frame, block):
        for side, column in ((0, width - 1), (1, 0)):
            picked = jnp.concatenate([block[r, column : column + 1] for r in range(height)], axis=0)
            edges[layer, frame, side, 0:height] = picked[:, :128].astype(jnp.bfloat16)
            edges[layer, frame, side, height : 2 * height, 0 : channels - 128] = picked[:, 128:].astype(jnp.bfloat16)

    def send(layer, frame, which):
        order = sorted(filter(which, around), key=lambda o: (o[0], o[1] != 0, o[2] == 0))
        for offsets in order:
            guarded(exists(position, sizes, offsets), lambda o=offsets: piece(layer, frame, packs.at[layer, frame], o).start())

    def level_side(offsets):
        return offsets[0] == 0

    def above(offsets):
        return offsets[0] == 1 and offsets[1] == 0

    def across(offsets):
        return offsets[0] == 1 and offsets[1] != 0

    def receive(layer, slot, main, which):
        for offsets in around:
            if not which(*offsets):
                continue
            back = tuple(-o for o in offsets)
            guarded(exists(position, sizes, back), lambda o=offsets: piece(layer, slot % frames, main, o).wait_recv())

    def shifts(block, first, last):
        column = lax.broadcasted_iota(jnp.int32, block.shape, 1)
        before = jnp.where(column == 0, first, pltpu.roll(block, 1, 1))
        after = jnp.where(column == width - 1, last, pltpu.roll(block, width - 1, 1))
        return [part.astype(jnp.bfloat16) for part in (before, block, after)]

    def fill_taps(slot, shifted):
        pieces = [shifted[x][y : y + height].reshape(cells, channels) for y in range(3) for x in range(3)]
        taps[slot] = jnp.concatenate(pieces, axis=-1)

    def column_of(layer, slot, k, side):
        tile = tiles[layer, slot, k, side].astype(jnp.float32)
        return jnp.concatenate([tile[:height], tile[height : 2 * height, : channels - 128]], axis=-1)

    def gather(layer, slot):
        source = packs[layer, slot - frames] if slot >= frames else mains[layer, slot]
        block = unpack(source, width).astype(jnp.float32)
        halo = []
        for side in range(2):
            level = column_of(layer, slot, 1, side)
            halo.append(jnp.stack([level[r : r + 1] for r in range(height)], axis=0))
        blank = jnp.zeros((1, width, channels), jnp.bfloat16)
        fill_taps(slot, [jnp.concatenate([blank, part, blank], axis=0) for part in shifts(block, *halo)])

    def edge_taps(layer, slot, k):
        block = unpack(rows[layer, slot, k][None], width).astype(jnp.float32)
        pick = slice(height - 1, height) if k == 0 else slice(0, 1)
        halo = [column_of(layer, slot, 2 * k, side)[pick][None] for side in range(2)]
        return jnp.concatenate(shifts(block, *halo), axis=-1)[0]

    def add_edges(layer, *terms):
        for k, ds in ((0, 1), (1, -1)):

            def correct(k=k):
                span = pl.ds(6 * k * channels, 3 * channels)
                line = pl.ds(k * (height - 1) * width, width)
                edge = {slot: edge_taps(layer, slot, k) for slot in {slot: 0 for _, slot, _ in terms}}
                for frame, slot, offset_t in terms:
                    acc[frame, line] += jnp.dot(edge[slot], weights[layer, offset_t, span], preferred_element_type=jnp.float32)

            guarded(exists(position, sizes, (0, -ds, 0)), correct)

    def dot(layer, slot, offset_t, span=slice(None)):
        return jnp.dot(taps[slot, span], weights[layer, offset_t], preferred_element_type=jnp.float32)

    halves = (slice(0, cells // 2), slice(cells // 2, cells))

    def add(layer, frame, slot, offset_t):
        for span in halves:
            acc[frame, span] += dot(layer, slot, offset_t, span)

    def finish(convolved, layer):
        mean_square = jnp.sum(convolved * convolved, axis=-1, keepdims=True) * (1.0 / channels)
        normed = convolved * lax.rsqrt(mean_square + 1e-06) * scales[layer]
        return (normed / (1.0 + jnp.exp(-normed))).reshape(height, width, channels)

    for frame in (1, 0):
        x_loads[frame].wait()
        if frame == 0:
            for copy in [*loads.values(), *scale_loads]:
                copy.start()
        packs[0, frame] = pack(x_ref[frame])
        fill_edges(0, frame, x_ref[frame].astype(jnp.float32))

    count = jnp.int32(0)
    for offsets in near:
        condition = exists(position, sizes, offsets)
        if condition is not None:
            count = count + (1 if condition is True else condition.astype(jnp.int32))
    pl.semaphore_wait(barrier, count)

    corners = [(1, -1, 0), (1, 1, 0)]
    send(0, 1, level_side)
    send(0, 1, above)
    for offsets in corners:
        guarded(
            exists(position, sizes, offsets),
            lambda o=offsets: pl.semaphore_signal(ready, inc=1, device_id=at((0, o[1], 0)), device_id_type=MESH),
        )
    send(0, 0, level_side)
    for offsets in corners:
        guarded(exists(position, sizes, offsets), lambda: pl.semaphore_wait(ready, 1))
    send(0, 1, across)
    send(0, 0, above)
    send(0, 0, across)

    def zero(ref, condition):
        def clear():
            ref[...] = jnp.zeros_like(ref)

        if condition is None:
            clear()
        elif condition is not True:
            pl.when(jnp.logical_not(condition))(clear)

    for layer in range(2):
        for slot in range(2 * frames):
            dz = 1 if slot < frames else 0
            if dz:
                zero(mains.at[layer, slot], exists(position, sizes, (-1, 0, 0)))
            for k, ds in ((0, 1), (1, -1)):
                zero(rows.at[layer, slot, k], exists(position, sizes, (-dz, -ds, 0)))
            for k in range(3):
                for side, db in ((0, 1), (1, -1)):
                    zero(tiles.at[layer, slot, k, side], exists(position, sizes, (-dz, k - 1, -db)))
    for copy in scale_loads:
        copy.wait()

    def level_in(layer, slot):
        dz = 1 if slot < frames else 0
        source = mains.at[layer, slot] if dz else packs.at[layer, slot - frames]
        receive(layer, slot, source, lambda z, y, x: (z, y) == (dz, 0))
        gather(layer, slot)

    def edges_in(layer, *slots):
        for slot in slots:
            dz = 1 if slot < frames else 0
            source = mains.at[layer, slot] if dz else packs.at[layer, slot - frames]
            receive(layer, slot, source, lambda z, y, x: z == dz and y != 0)

    def emit_hidden(frame, values):
        packs[1, frame] = pack(values).astype(jnp.bfloat16)
        fill_edges(1, frame, values)
        for which in (level_side, above, across):
            send(1, frame, which)

    def emit_output(frame, values):
        out_ref[frame] = values.astype(jnp.bfloat16)

    loads[0, 2].wait()
    loads[0, 1].wait()
    level_in(0, 3)
    level_in(0, 2)
    acc[1] = dot(0, 3, 2)
    acc[0] = dot(0, 2, 2)
    add(0, 1, 2, 1)
    edges_in(0, 3, 2)
    add_edges(0, (1, 3, 2), (0, 2, 2), (1, 2, 1))
    loads[0, 0].wait()
    level_in(0, 1)
    add(0, 1, 1, 0)
    wait_sent(0, 1)
    edges_in(0, 1)
    add_edges(0, (1, 1, 0))
    emit_hidden(1, finish(acc[1], 0))
    add(0, 0, 1, 1)
    add_edges(0, (0, 1, 1))
    level_in(0, 0)
    add(0, 0, 0, 0)
    wait_sent(0, 0)
    edges_in(0, 0)
    add_edges(0, (0, 0, 0))
    emit_hidden(0, finish(acc[0], 0))

    loads[1].wait()
    level_in(1, 3)
    for span in halves:
        acc[1, span] = dot(1, 3, 2, span)
    level_in(1, 2)
    acc[0] = dot(1, 2, 2)
    acc[1] += dot(1, 2, 1)
    level_in(1, 1)
    acc[0] += dot(1, 1, 1)
    acc[1] += dot(1, 1, 0)
    edges_in(1, 3, 2, 1)
    add_edges(1, (1, 3, 2), (0, 2, 2), (1, 2, 1), (1, 1, 0), (0, 1, 1))
    emit_output(1, finish(acc[1], 1))
    level_in(1, 0)
    add(1, 0, 0, 0)
    edges_in(1, 0)
    add_edges(1, (0, 0, 0))
    emit_output(0, finish(acc[0], 1))

    for frame in (1, 0):
        wait_sent(1, frame)


def shards(sizes, frames_in, weight_first, scale_first, weight_second, scale_second):
    frames, height, width, channels = frames_in.shape
    anywhere = pl.BlockSpec(memory_space=pl.ANY)
    lines = width * channels // 128
    flat = (3, 9 * channels, channels)
    half = jnp.bfloat16
    kinds = kind_counts(sizes)[1]
    return pl.pallas_call(
        functools.partial(kernel, sizes),
        out_shape=pltpu.VMEM(frames_in.shape, half),
        in_specs=[anywhere] * 5,
        out_specs=pl.BlockSpec(memory_space=pltpu.VMEM),
        scratch_shapes=[
            pltpu.VMEM(frames_in.shape, half),
            pltpu.VMEM((2, 1, channels), jnp.float32),
            pltpu.VMEM((2, *flat), half),
            pltpu.VMEM((2, frames, height, lines, 128), half),
            pltpu.VMEM((2, frames, 2, 2 * height, 128), half),
            pltpu.VMEM((2, frames, height, lines, 128), half),
            pltpu.VMEM((2, 2 * frames, 2, lines, 128), half),
            pltpu.VMEM((2, 2 * frames, 3, 2, 2 * height, 128), half),
            pltpu.VMEM((2 * frames, height * width, 9 * channels), half),
            pltpu.VMEM((frames, height * width, channels), jnp.float32),
            pltpu.SemaphoreType.DMA((6,)),
            pltpu.SemaphoreType.DMA((frames * kinds,)),
            pltpu.SemaphoreType.DMA((2, frames * kinds)),
            pltpu.SemaphoreType.REGULAR,
        ],
        compiler_params=pltpu.CompilerParams(collective_id=0, has_side_effects=True),
        name="conv_block",
    )(
        frames_in,
        weight_first.reshape(flat),
        scale_first.reshape(1, channels),
        weight_second.reshape(flat),
        scale_second.reshape(1, channels),
    )


def solution(mesh):
    sizes = tuple(mesh.shape[axis] for axis in AXES)
    return jax.shard_map(
        functools.partial(shards, sizes),
        mesh=mesh,
        in_specs=(P(("groups", "frame"), "strip", "slab", None), P(), P(), P(), P()),
        out_specs=P(("groups", "frame"), "strip", "slab", None),
        check_vma=False,
    )
```

```python
import functools

import jax
import jax.numpy as jnp
from jax import lax
from jax.experimental import pallas as pl
from jax.experimental.pallas import tpu as pltpu
from jax.sharding import PartitionSpec as P

MESH = pl.DeviceIdType.MESH
AXES = ("frame", "strip", "slab")


def exists(position, sizes, offsets):
    checks = []
    for index, size, offset in zip(position, sizes, offsets):
        if abs(offset) >= size:
            return None
        if offset > 0:
            checks.append(index < size - offset)
        elif offset < 0:
            checks.append(index >= -offset)
    return functools.reduce(jnp.logical_and, checks) if checks else True


def guarded(condition, action):
    if condition is None:
        return
    if condition is True:
        action()
    else:
        pl.when(condition)(action)


def ways(sizes):
    return tuple(2 if size > 2 else 1 for size in sizes[1:])


def kind_counts(sizes):
    strips, slabs = ways(sizes)
    mains = min(sizes[1], 3)
    late = mains + slabs + strips + strips * slabs
    return mains, late, 2 * late - mains


def pack(block):
    lead, half = 128, block.shape[1] // 2
    rest = block[..., lead:]
    return jnp.concatenate([block[..., :lead], jnp.concatenate([rest[:, :half], rest[:, half:]], axis=-1)], axis=1)


def unpack(packed, width):
    rest, lanes = packed[:, width:], packed.shape[-1] // 2
    rest = jnp.concatenate([rest[..., :lanes], rest[..., lanes:]], axis=1)
    return jnp.concatenate([packed[:, :width], rest], axis=-1)


def kernel(
    sizes,
    x_hbm,
    w1_hbm,
    s1_hbm,
    w2_hbm,
    s2_hbm,
    out_ref,
    x_ref,
    scales,
    weights,
    packs,
    edges,
    mains,
    rows,
    tiles,
    taps,
    acc,
    local_sem,
    send_sem,
    recv_sem,
    ready,
):
    frames, height, width, channels = x_ref.shape
    cells = height * width
    position = tuple(lax.axis_index(axis) for axis in AXES)

    def at(offsets):
        return {axis: index + offset for axis, index, offset in zip(AXES, position, offsets)}

    around = [(dz, ds, db) for dz in (0, 1) for ds in (-1, 0, 1) for db in (-1, 0, 1) if (dz, ds, db) != (0, 0, 0)]

    near = [offsets for offsets in around if not (offsets[0] and offsets[1])]

    barrier = pltpu.get_barrier_semaphore()
    for offsets in near:
        back = tuple(-o for o in offsets)
        guarded(
            exists(position, sizes, back),
            lambda back=back: pl.semaphore_signal(barrier, inc=1, device_id=at(back), device_id_type=MESH),
        )

    x_loads = [pltpu.make_async_copy(x_hbm.at[frame], x_ref.at[frame], local_sem.at[frame]) for frame in range(frames)]
    for frame in reversed(range(frames)):
        x_loads[frame].start()

    loads = {(0, t): pltpu.make_async_copy(w1_hbm.at[t], weights.at[0, t], local_sem.at[t]) for t in (2, 1, 0)}
    loads[1] = pltpu.make_async_copy(w2_hbm, weights.at[1], local_sem.at[3])
    scale_loads = [pltpu.make_async_copy(ref, scales.at[layer], local_sem.at[4 + layer]) for layer, ref in enumerate((s1_hbm, s2_hbm))]

    strips, slabs = ways(sizes)
    mains_in, late_kinds, kinds = kind_counts(sizes)
    if mains_in == 1:
        parts = [pl.ds(0, height)]
    elif mains_in == 2:
        parts = [pl.ds(position[1], height - 1), pl.ds((1 - position[1]) * (height - 1), 1)]
    else:
        parts = [pl.ds(1, height - 2), pl.ds(0, 1), pl.ds(height - 1, 1)]
    beside = [offsets for offsets in around if offsets != (1, 0, 0)]

    def remote(layer, index, src, dst, offsets):
        return pltpu.make_async_remote_copy(
            src_ref=src,
            dst_ref=dst,
            send_sem=send_sem.at[index],
            recv_sem=recv_sem.at[layer, index],
            device_id=at(offsets),
            device_id_type=MESH,
        )

    def main_part(layer, frame, part):
        span = parts[part]
        return remote(layer, frame * kinds + part, packs.at[layer, frame, span], mains.at[layer, frame, span], (1, 0, 0))

    relayed = ((0, 1),)

    def passed(layer, frame, offsets):
        return (layer, frame) in relayed and across(offsets)

    def sends(layer, frame, offsets):
        dz, ds, db = offsets
        return exists(position, sizes, (-1, ds, -db) if passed(layer, frame, offsets) else offsets)

    def piece(layer, frame, offsets):
        dz, ds, db = offsets
        slot = frame if dz else frames + frame
        k = 0 if ds > 0 else 1
        side = 0 if db > 0 else 1
        if db == 0:
            row = height - 1 if ds > 0 else 0
            src, dst = (mains if passed(layer, frame, offsets) else packs).at[layer, frame, row], rows.at[layer, slot, k]
            kind = slabs + k % strips
        else:
            src = tiles.at[layer, frame, 1, side] if passed(layer, frame, offsets) else edges.at[layer, frame, side]
            dst = tiles.at[layer, slot, 1 - ds, side]
            kind = side % slabs if ds == 0 else slabs + strips + (k % strips) * slabs + side % slabs
        index = frame * kinds + kind + (mains_in if dz else late_kinds)
        return remote(layer, index, src, dst, (0, ds, 0) if passed(layer, frame, offsets) else offsets)

    def wait_sent(layer, frame):
        for part in range(mains_in):
            guarded(exists(position, sizes, (1, 0, 0)), lambda p=part: main_part(layer, frame, p).wait_send())
        for offsets in beside:
            guarded(sends(layer, frame, offsets), lambda o=offsets: piece(layer, frame, o).wait_send())

    def fill_edges(layer, frame, block, first=0):
        for side, column in ((0, width - 1), (1, 0)):
            picked = jnp.concatenate([block[r, column : column + 1] for r in range(block.shape[0])], axis=0)
            last = first + block.shape[0]
            edges[layer, frame, side, first:last] = picked[:, :128].astype(jnp.bfloat16)
            edges[layer, frame, side, height + first : height + last, 0 : channels - 128] = picked[:, 128:].astype(jnp.bfloat16)

    def send(layer, frame, which):
        order = sorted(filter(which, beside), key=lambda o: (o[0], o[1] != 0, o[2] != 0))
        for offsets in order:
            guarded(sends(layer, frame, offsets), lambda o=offsets: piece(layer, frame, o).start())

    def send_main(layer, frame, *chosen):
        for part in chosen:
            guarded(exists(position, sizes, (1, 0, 0)), lambda p=part: main_part(layer, frame, p).start())

    def level_side(offsets):
        return offsets[0] == 0

    def above(offsets):
        return offsets[0] == 1 and offsets[1] == 0

    def across(offsets):
        return offsets[0] == 1 and offsets[1] != 0

    def receive(layer, frame, which):
        for offsets in filter(which, beside):
            back = tuple(-o for o in offsets)
            guarded(exists(position, sizes, back), lambda o=offsets: piece(layer, frame, o).wait_recv())

    def receive_main(layer, frame, *chosen):
        for part in chosen:
            guarded(exists(position, sizes, (-1, 0, 0)), lambda p=part: main_part(layer, frame, p).wait_recv())

    rim = range(1, mains_in)

    def pass_on(layer, frame):
        if (layer, frame) not in relayed:
            return
        receive_main(layer, frame, *rim)
        receive(layer, frame, above)
        send(layer, frame, across)

    def shifts(block, first, last):
        column = lax.broadcasted_iota(jnp.int32, block.shape, 1)
        before = jnp.where(column == 0, first, pltpu.roll(block, 1, 1))
        after = jnp.where(column == width - 1, last, pltpu.roll(block, width - 1, 1))
        return [part.astype(jnp.bfloat16) for part in (before, block, after)]

    def fill_taps(slot, shifted):
        pieces = [shifted[x][y : y + height].reshape(cells, channels) for y in range(3) for x in range(3)]
        taps[slot] = jnp.concatenate(pieces, axis=-1)

    def column_of(layer, slot, k, side):
        tile = tiles[layer, slot, k, side].astype(jnp.float32)
        return jnp.concatenate([tile[:height], tile[height : 2 * height, : channels - 128]], axis=-1)

    def gather(layer, slot):
        source = packs[layer, slot - frames] if slot >= frames else mains[layer, slot]
        block = unpack(source, width).astype(jnp.float32)
        halo = []
        for side in range(2):
            level = column_of(layer, slot, 1, side)
            halo.append(jnp.stack([level[r : r + 1] for r in range(height)], axis=0))
        blank = jnp.zeros((1, width, channels), jnp.bfloat16)
        fill_taps(slot, [jnp.concatenate([blank, part, blank], axis=0) for part in shifts(block, *halo)])

    def edge_taps(layer, slot, k):
        block = unpack(rows[layer, slot, k][None], width).astype(jnp.float32)
        pick = slice(height - 1, height) if k == 0 else slice(0, 1)
        halo = [column_of(layer, slot, 2 * k, side)[pick][None] for side in range(2)]
        return jnp.concatenate(shifts(block, *halo), axis=-1)[0]

    bounds = tuple((k, exists(position, sizes, (0, ds, 0))) for k, ds in ((0, -1), (1, 1)))

    def correct(layer, k, terms):
        span = pl.ds(6 * k * channels, 3 * channels)
        line = pl.ds(k * (height - 1) * width, width)
        edge = {slot: edge_taps(layer, slot, k) for slot in {slot: 0 for _, slot, _ in terms}}
        for frame, slot, offset_t in terms:
            acc[frame, line] += jnp.dot(edge[slot], weights[layer, offset_t, span], preferred_element_type=jnp.float32)

    def add_edges(layer, *terms):
        for k, beside in bounds:
            guarded(beside, lambda k=k: correct(layer, k, terms))

    def settle_edges(layer, frame, *terms):
        def step(k):
            correct(layer, k, terms)
            settle(layer, frame, k * (height - 1), k * (height - 1) + 1)

        for k, beside in bounds:
            guarded(beside, lambda k=k: step(k))

    def dot(layer, slot, offset_t, span=slice(None)):
        return jnp.dot(taps[slot, span], weights[layer, offset_t], preferred_element_type=jnp.float32)

    halves = (slice(0, cells // 2), slice(cells // 2, cells))

    def add(layer, frame, slot, offset_t):
        for span in halves:
            acc[frame, span] += dot(layer, slot, offset_t, span)

    def finish(convolved, layer):
        mean_square = jnp.sum(convolved * convolved, axis=-1, keepdims=True) * (1.0 / channels)
        normed = convolved * lax.rsqrt(mean_square + 1e-06) * scales[layer]
        return (normed / (1.0 + jnp.exp(-normed))).reshape(-1, width, channels)

    def settle(layer, frame, first, last):
        values = finish(acc[frame, first * width : last * width], layer)
        if layer == 0:
            packs[1, frame, first:last] = pack(values).astype(jnp.bfloat16)
            fill_edges(1, frame, values, first)
        else:
            out_ref[frame, first:last] = values.astype(jnp.bfloat16)

    for frame in (1, 0):
        x_loads[frame].wait()
        if frame == 0:
            for copy in [*loads.values(), *scale_loads]:
                copy.start()
        packs[0, frame] = pack(x_ref[frame])
        fill_edges(0, frame, x_ref[frame].astype(jnp.float32))

    count = jnp.int32(0)
    for offsets in near:
        condition = exists(position, sizes, offsets)
        if condition is not None:
            count = count + (1 if condition is True else condition.astype(jnp.int32))
    pl.semaphore_wait(barrier, count)

    corners = [(1, -1, 0), (1, 1, 0)]
    send(0, 1, level_side)
    send_main(0, 1, *rim)
    send(0, 1, above)
    send_main(0, 1, 0)
    for offsets in corners:
        guarded(
            exists(position, sizes, offsets),
            lambda o=offsets: pl.semaphore_signal(ready, inc=1, device_id=at((0, o[1], 0)), device_id_type=MESH),
        )
    send(0, 0, level_side)
    if (0, 1) in relayed:
        send_main(0, 0, 0, *rim)
        send(0, 0, above)
    for offsets in corners:
        guarded(exists(position, sizes, offsets), lambda: pl.semaphore_wait(ready, 1))
    if (0, 1) not in relayed:
        send(0, 1, across)
        send_main(0, 0, 0, *rim)
        send(0, 0, above)
    send(0, 0, across)

    def zero(ref, condition):
        def clear():
            ref[...] = jnp.zeros_like(ref)

        if condition is None:
            clear()
        elif condition is not True:
            pl.when(jnp.logical_not(condition))(clear)

    for layer in range(2):
        for slot in range(2 * frames):
            dz = 1 if slot < frames else 0
            if dz:
                zero(mains.at[layer, slot], exists(position, sizes, (-1, 0, 0)))
            for k, ds in ((0, 1), (1, -1)):
                zero(rows.at[layer, slot, k], exists(position, sizes, (-dz, -ds, 0)))
            for k in range(3):
                for side, db in ((0, 1), (1, -1)):
                    zero(tiles.at[layer, slot, k, side], exists(position, sizes, (-dz, k - 1, -db)))
    for copy in scale_loads:
        copy.wait()

    def level_in(layer, slot):
        if slot >= frames:
            receive(layer, slot - frames, lambda o: o[0] == 0 and o[1] == 0)
        elif (layer, slot) in relayed:
            receive_main(layer, slot, 0)
        else:
            receive_main(layer, slot, 0, *rim)
            receive(layer, slot, above)

    def edges_in(layer, *slots):
        for slot in slots:
            dz = 1 if slot < frames else 0
            receive(layer, slot % frames, lambda o: o[0] == dz and o[1] != 0)

    def send_hidden(frame):
        send(1, frame, level_side)
        if (1, frame) not in relayed:
            send(1, frame, across)
        send_main(1, frame, *rim)
        send(1, frame, above)

    loads[0, 2].wait()
    loads[0, 1].wait()
    level_in(0, 3)
    level_in(0, 2)
    gather(0, 3)
    gather(0, 2)
    acc[1] = dot(0, 3, 2)
    acc[0] = dot(0, 2, 2)
    add(0, 1, 2, 1)
    pass_on(0, 1)
    edges_in(0, 3, 2)
    add_edges(0, (1, 3, 2), (0, 2, 2), (1, 2, 1))
    loads[0, 0].wait()
    level_in(0, 1)
    gather(0, 1)
    add(0, 1, 1, 0)
    settle(0, 1, 0, height)
    wait_sent(0, 1)
    send_main(1, 1, 0)
    edges_in(0, 1)
    settle_edges(0, 1, (1, 1, 0))
    send_hidden(1)
    add(0, 0, 1, 1)
    add_edges(0, (0, 1, 1))
    level_in(0, 0)
    gather(0, 0)
    add(0, 0, 0, 0)
    settle(0, 0, 0, height)
    wait_sent(0, 0)
    send_main(1, 0, 0)
    edges_in(0, 0)
    settle_edges(0, 0, (0, 0, 0))
    send_hidden(0)

    loads[1].wait()
    level_in(1, 3)
    gather(1, 3)
    for span in halves:
        acc[1, span] = dot(1, 3, 2, span)
    pass_on(1, 1)
    level_in(1, 2)
    level_in(1, 1)
    gather(1, 2)
    gather(1, 1)
    acc[0] = dot(1, 2, 2)
    acc[1] += dot(1, 2, 1)
    acc[0] += dot(1, 1, 1)
    acc[1] += dot(1, 1, 0)
    settle(1, 1, 0, height)
    edges_in(1, 3, 2, 1)
    settle_edges(1, 1, (1, 3, 2), (0, 2, 2), (1, 2, 1), (1, 1, 0), (0, 1, 1))
    level_in(1, 0)
    gather(1, 0)
    add(1, 0, 0, 0)
    settle(1, 0, 0, height)
    edges_in(1, 0)
    settle_edges(1, 0, (0, 0, 0))

    for frame in (1, 0):
        wait_sent(1, frame)


def shards(sizes, frames_in, weight_first, scale_first, weight_second, scale_second):
    frames, height, width, channels = frames_in.shape
    anywhere = pl.BlockSpec(memory_space=pl.ANY)
    lines = width * channels // 128
    flat = (3, 9 * channels, channels)
    half = jnp.bfloat16
    kinds = kind_counts(sizes)[2]
    return pl.pallas_call(
        functools.partial(kernel, sizes),
        out_shape=pltpu.VMEM(frames_in.shape, half),
        in_specs=[anywhere] * 5,
        out_specs=pl.BlockSpec(memory_space=pltpu.VMEM),
        scratch_shapes=[
            pltpu.VMEM(frames_in.shape, half),
            pltpu.VMEM((2, 1, channels), jnp.float32),
            pltpu.VMEM((2, *flat), half),
            pltpu.VMEM((2, frames, height, lines, 128), half),
            pltpu.VMEM((2, frames, 2, 2 * height, 128), half),
            pltpu.VMEM((2, frames, height, lines, 128), half),
            pltpu.VMEM((2, 2 * frames, 2, lines, 128), half),
            pltpu.VMEM((2, 2 * frames, 3, 2, 2 * height, 128), half),
            pltpu.VMEM((2 * frames, height * width, 9 * channels), half),
            pltpu.VMEM((frames, height * width, channels), jnp.float32),
            pltpu.SemaphoreType.DMA((6,)),
            pltpu.SemaphoreType.DMA((frames * kinds,)),
            pltpu.SemaphoreType.DMA((2, frames * kinds)),
            pltpu.SemaphoreType.REGULAR,
        ],
        compiler_params=pltpu.CompilerParams(collective_id=0, has_side_effects=True),
        name="conv_block",
    )(
        frames_in,
        weight_first.reshape(flat),
        scale_first.reshape(1, channels),
        weight_second.reshape(flat),
        scale_second.reshape(1, channels),
    )


def solution(mesh):
    sizes = tuple(mesh.shape[axis] for axis in AXES)
    return jax.shard_map(
        functools.partial(shards, sizes),
        mesh=mesh,
        in_specs=(P(("groups", "frame"), "strip", "slab", None), P(), P(), P(), P()),
        out_specs=P(("groups", "frame"), "strip", "slab", None),
        check_vma=False,
    )
```

```python
import functools

import jax
import jax.numpy as jnp
from jax import lax
from jax.experimental import pallas as pl
from jax.experimental.pallas import tpu as pltpu
from jax.sharding import PartitionSpec as P

MESH = pl.DeviceIdType.MESH
AXES = ("frame", "strip", "slab")


def exists(position, sizes, offsets):
    checks = []
    for index, size, offset in zip(position, sizes, offsets):
        if abs(offset) >= size:
            return None
        if offset > 0:
            checks.append(index < size - offset)
        elif offset < 0:
            checks.append(index >= -offset)
    return functools.reduce(jnp.logical_and, checks) if checks else True


def guarded(condition, action):
    if condition is None:
        return
    if condition is True:
        action()
    else:
        pl.when(condition)(action)


def ways(sizes):
    return tuple(2 if size > 2 else 1 for size in sizes[1:])


def kind_counts(sizes):
    strips, slabs = ways(sizes)
    mains = min(sizes[1], 3)
    late = mains + slabs + strips + strips * slabs
    return mains, late, 2 * late - mains


def pack(block):
    lead, half = 128, block.shape[1] // 2
    rest = block[..., lead:]
    return jnp.concatenate([block[..., :lead], jnp.concatenate([rest[:, :half], rest[:, half:]], axis=-1)], axis=1)


def unpack(packed, width):
    rest, lanes = packed[:, width:], packed.shape[-1] // 2
    rest = jnp.concatenate([rest[..., :lanes], rest[..., lanes:]], axis=1)
    return jnp.concatenate([packed[:, :width], rest], axis=-1)


def kernel(
    sizes,
    x_hbm,
    w1_hbm,
    s1_hbm,
    w2_hbm,
    s2_hbm,
    out_ref,
    x_ref,
    scales,
    weights,
    packs,
    edges,
    mains,
    rows,
    tiles,
    taps,
    acc,
    local_sem,
    send_sem,
    recv_sem,
    ready,
):
    frames, height, width, channels = x_ref.shape
    cells = height * width
    position = tuple(lax.axis_index(axis) for axis in AXES)

    def at(offsets):
        return {axis: index + offset for axis, index, offset in zip(AXES, position, offsets)}

    around = [(dz, ds, db) for dz in (0, 1) for ds in (-1, 0, 1) for db in (-1, 0, 1) if (dz, ds, db) != (0, 0, 0)]

    near = [offsets for offsets in around if not (offsets[0] and offsets[1])]

    barrier = pltpu.get_barrier_semaphore()
    for offsets in near:
        back = tuple(-o for o in offsets)
        guarded(
            exists(position, sizes, back),
            lambda back=back: pl.semaphore_signal(barrier, inc=1, device_id=at(back), device_id_type=MESH),
        )

    x_loads = [pltpu.make_async_copy(x_hbm.at[frame], x_ref.at[frame], local_sem.at[frame]) for frame in range(frames)]
    for frame in reversed(range(frames)):
        x_loads[frame].start()

    loads = {(0, t): pltpu.make_async_copy(w1_hbm.at[t], weights.at[0, t], local_sem.at[t]) for t in (2, 1, 0)}
    loads[1] = pltpu.make_async_copy(w2_hbm, weights.at[1], local_sem.at[3])
    scale_loads = [pltpu.make_async_copy(ref, scales.at[layer], local_sem.at[4 + layer]) for layer, ref in enumerate((s1_hbm, s2_hbm))]

    strips, slabs = ways(sizes)
    mains_in, late_kinds, kinds = kind_counts(sizes)
    if mains_in == 1:
        parts = [pl.ds(0, height)]
    elif mains_in == 2:
        parts = [pl.ds(position[1], height - 1), pl.ds((1 - position[1]) * (height - 1), 1)]
    else:
        parts = [pl.ds(1, height - 2), pl.ds(0, 1), pl.ds(height - 1, 1)]
    beside = [offsets for offsets in around if offsets != (1, 0, 0)]

    def remote(layer, index, src, dst, offsets):
        return pltpu.make_async_remote_copy(
            src_ref=src,
            dst_ref=dst,
            send_sem=send_sem.at[index],
            recv_sem=recv_sem.at[layer, index],
            device_id=at(offsets),
            device_id_type=MESH,
        )

    def main_part(layer, frame, part):
        span = parts[part]
        return remote(layer, frame * kinds + part, packs.at[layer, frame, span], mains.at[layer, frame, span], (1, 0, 0))

    relayed = ((0, 1),)

    def passed(layer, frame, offsets):
        return (layer, frame) in relayed and across(offsets)

    def sends(layer, frame, offsets):
        dz, ds, db = offsets
        return exists(position, sizes, (-1, ds, -db) if passed(layer, frame, offsets) else offsets)

    def piece(layer, frame, offsets):
        dz, ds, db = offsets
        slot = frame if dz else frames + frame
        k = 0 if ds > 0 else 1
        side = 0 if db > 0 else 1
        if db == 0:
            row = height - 1 if ds > 0 else 0
            src, dst = (mains if passed(layer, frame, offsets) else packs).at[layer, frame, row], rows.at[layer, slot, k]
            kind = slabs + k % strips
        else:
            src = tiles.at[layer, frame, 1, side] if passed(layer, frame, offsets) else edges.at[layer, frame, side]
            dst = tiles.at[layer, slot, 1 - ds, side]
            kind = side % slabs if ds == 0 else slabs + strips + (k % strips) * slabs + side % slabs
        index = frame * kinds + kind + (mains_in if dz else late_kinds)
        return remote(layer, index, src, dst, (0, ds, 0) if passed(layer, frame, offsets) else offsets)

    def wait_sent(layer, frame):
        for part in range(mains_in):
            guarded(exists(position, sizes, (1, 0, 0)), lambda p=part: main_part(layer, frame, p).wait_send())
        for offsets in beside:
            guarded(sends(layer, frame, offsets), lambda o=offsets: piece(layer, frame, o).wait_send())

    def fill_edges(layer, frame, block, first=0):
        for side, column in ((0, width - 1), (1, 0)):
            picked = jnp.concatenate([block[r, column : column + 1] for r in range(block.shape[0])], axis=0)
            last = first + block.shape[0]
            edges[layer, frame, side, first:last] = picked[:, :128].astype(jnp.bfloat16)
            edges[layer, frame, side, height + first : height + last, 0 : channels - 128] = picked[:, 128:].astype(jnp.bfloat16)

    def send(layer, frame, which):
        order = sorted(filter(which, beside), key=lambda o: (o[0], o[1] != 0, o[2] != 0))
        for offsets in order:
            guarded(sends(layer, frame, offsets), lambda o=offsets: piece(layer, frame, o).start())

    def send_main(layer, frame, *chosen):
        for part in chosen:
            guarded(exists(position, sizes, (1, 0, 0)), lambda p=part: main_part(layer, frame, p).start())

    def level_side(offsets):
        return offsets[0] == 0

    def above(offsets):
        return offsets[0] == 1 and offsets[1] == 0

    def across(offsets):
        return offsets[0] == 1 and offsets[1] != 0

    def receive(layer, frame, which):
        for offsets in filter(which, beside):
            back = tuple(-o for o in offsets)
            guarded(exists(position, sizes, back), lambda o=offsets: piece(layer, frame, o).wait_recv())

    def receive_main(layer, frame, *chosen):
        for part in chosen:
            guarded(exists(position, sizes, (-1, 0, 0)), lambda p=part: main_part(layer, frame, p).wait_recv())

    rim = range(1, mains_in)

    def pass_on(layer, frame):
        if (layer, frame) not in relayed:
            return
        receive_main(layer, frame, *rim)
        receive(layer, frame, above)
        send(layer, frame, across)

    def shifts(block, first, last):
        column = lax.broadcasted_iota(jnp.int32, block.shape, 1)
        before = jnp.where(column == 0, first, pltpu.roll(block, 1, 1))
        after = jnp.where(column == width - 1, last, pltpu.roll(block, width - 1, 1))
        return [part.astype(jnp.bfloat16) for part in (before, block, after)]

    def fill_taps(slot, shifted):
        pieces = [shifted[x][y : y + height].reshape(cells, channels) for y in range(3) for x in range(3)]
        taps[slot] = jnp.concatenate(pieces, axis=-1)

    def column_of(layer, slot, k, side):
        tile = tiles[layer, slot, k, side].astype(jnp.float32)
        return jnp.concatenate([tile[:height], tile[height : 2 * height, : channels - 128]], axis=-1)

    def gather(layer, slot):
        source = packs[layer, slot - frames] if slot >= frames else mains[layer, slot]
        block = unpack(source, width).astype(jnp.float32)
        halo = []
        for side in range(2):
            level = column_of(layer, slot, 1, side)
            halo.append(jnp.stack([level[r : r + 1] for r in range(height)], axis=0))
        blank = jnp.zeros((1, width, channels), jnp.bfloat16)
        fill_taps(slot, [jnp.concatenate([blank, part, blank], axis=0) for part in shifts(block, *halo)])

    def edge_taps(layer, slot, k):
        block = unpack(rows[layer, slot, k][None], width).astype(jnp.float32)
        pick = slice(height - 1, height) if k == 0 else slice(0, 1)
        halo = [column_of(layer, slot, 2 * k, side)[pick][None] for side in range(2)]
        return jnp.concatenate(shifts(block, *halo), axis=-1)[0]

    bounds = tuple((k, exists(position, sizes, (0, ds, 0))) for k, ds in ((0, -1), (1, 1)))

    def correct(layer, k, terms):
        span = pl.ds(6 * k * channels, 3 * channels)
        line = pl.ds(k * (height - 1) * width, width)
        edge = {slot: edge_taps(layer, slot, k) for slot in {slot: 0 for _, slot, _ in terms}}
        for frame, slot, offset_t in terms:
            acc[frame, line] += jnp.dot(edge[slot], weights[layer, offset_t, span], preferred_element_type=jnp.float32)

    def add_edges(layer, *terms):
        for k, beside in bounds:
            guarded(beside, lambda k=k: correct(layer, k, terms))

    def settle_edges(layer, frame, *terms):
        def step(k):
            correct(layer, k, terms)
            settle(layer, frame, k * (height - 1), k * (height - 1) + 1)

        for k, beside in bounds:
            guarded(beside, lambda k=k: step(k))

    def dot(layer, slot, offset_t, span=slice(None)):
        return jnp.dot(taps[slot, span], weights[layer, offset_t], preferred_element_type=jnp.float32)

    halves = (slice(0, cells // 2), slice(cells // 2, cells))

    def add(layer, frame, slot, offset_t):
        for span in halves:
            acc[frame, span] += dot(layer, slot, offset_t, span)

    def finish(convolved, layer):
        mean_square = jnp.sum(convolved * convolved, axis=-1, keepdims=True) * (1.0 / channels)
        normed = convolved * lax.rsqrt(mean_square + 1e-06) * scales[layer]
        return (normed / (1.0 + jnp.exp(-normed))).reshape(-1, width, channels)

    def settle(layer, frame, first, last):
        values = finish(acc[frame, first * width : last * width], layer)
        if layer == 0:
            packs[1, frame, first:last] = pack(values).astype(jnp.bfloat16)
            fill_edges(1, frame, values, first)
        else:
            out_ref[frame, first:last] = values.astype(jnp.bfloat16)

    for frame in (1, 0):
        x_loads[frame].wait()
        if frame == 0:
            for copy in [*loads.values(), *scale_loads]:
                copy.start()
        packs[0, frame] = pack(x_ref[frame])
        fill_edges(0, frame, x_ref[frame].astype(jnp.float32))

    count = jnp.int32(0)
    for offsets in near:
        condition = exists(position, sizes, offsets)
        if condition is not None:
            count = count + (1 if condition is True else condition.astype(jnp.int32))
    pl.semaphore_wait(barrier, count)

    corners = [(1, -1, 0), (1, 1, 0)]
    send(0, 1, level_side)
    send_main(0, 1, *rim)
    send(0, 1, above)
    send_main(0, 1, 0)
    for offsets in corners:
        guarded(
            exists(position, sizes, offsets),
            lambda o=offsets: pl.semaphore_signal(ready, inc=1, device_id=at((0, o[1], 0)), device_id_type=MESH),
        )
    send(0, 0, level_side)
    if (0, 1) in relayed:
        send_main(0, 0, 0, *rim)
        send(0, 0, above)
    for offsets in corners:
        guarded(exists(position, sizes, offsets), lambda: pl.semaphore_wait(ready, 1))
    if (0, 1) not in relayed:
        send(0, 1, across)
        send_main(0, 0, 0, *rim)
        send(0, 0, above)
    send(0, 0, across)

    def zero(ref, condition):
        def clear():
            ref[...] = jnp.zeros_like(ref)

        if condition is None:
            clear()
        elif condition is not True:
            pl.when(jnp.logical_not(condition))(clear)

    for layer in range(2):
        for slot in range(2 * frames):
            dz = 1 if slot < frames else 0
            if dz:
                zero(mains.at[layer, slot], exists(position, sizes, (-1, 0, 0)))
            for k, ds in ((0, 1), (1, -1)):
                zero(rows.at[layer, slot, k], exists(position, sizes, (-dz, -ds, 0)))
            for k in range(3):
                for side, db in ((0, 1), (1, -1)):
                    zero(tiles.at[layer, slot, k, side], exists(position, sizes, (-dz, k - 1, -db)))
    for copy in scale_loads:
        copy.wait()

    def level_in(layer, slot):
        if slot >= frames:
            receive(layer, slot - frames, lambda o: o[0] == 0 and o[1] == 0)
        elif (layer, slot) in relayed:
            receive_main(layer, slot, 0)
        else:
            receive_main(layer, slot, 0, *rim)
            receive(layer, slot, above)

    def edges_in(layer, *slots):
        for slot in slots:
            dz = 1 if slot < frames else 0
            receive(layer, slot % frames, lambda o: o[0] == dz and o[1] != 0)

    def send_hidden(frame):
        send(1, frame, level_side)
        if (1, frame) not in relayed:
            send(1, frame, across)
        send_main(1, frame, *rim)
        send(1, frame, above)

    loads[0, 2].wait()
    loads[0, 1].wait()
    level_in(0, 3)
    level_in(0, 2)
    gather(0, 3)
    gather(0, 2)
    acc[1] = dot(0, 3, 2)
    acc[0] = dot(0, 2, 2)
    pass_on(0, 1)
    add(0, 1, 2, 1)
    edges_in(0, 3, 2)
    add_edges(0, (1, 3, 2), (0, 2, 2), (1, 2, 1))
    loads[0, 0].wait()
    level_in(0, 1)
    gather(0, 1)
    add(0, 1, 1, 0)
    settle(0, 1, 0, height)
    wait_sent(0, 1)
    send_main(1, 1, 0)
    add(0, 0, 1, 1)
    edges_in(0, 1)
    settle_edges(0, 1, (1, 1, 0))
    send_hidden(1)
    level_in(0, 0)
    gather(0, 0)
    add(0, 0, 0, 0)
    settle(0, 0, 0, height)
    wait_sent(0, 0)
    send_main(1, 0, 0)
    edges_in(0, 0)
    settle_edges(0, 0, (0, 0, 0), (0, 1, 1))
    send_hidden(0)

    loads[1].wait()
    level_in(1, 3)
    gather(1, 3)
    for span in halves:
        acc[1, span] = dot(1, 3, 2, span)
    pass_on(1, 1)
    level_in(1, 2)
    level_in(1, 1)
    gather(1, 2)
    gather(1, 1)
    acc[0] = dot(1, 2, 2)
    acc[1] += dot(1, 2, 1)
    acc[0] += dot(1, 1, 1)
    acc[1] += dot(1, 1, 0)
    settle(1, 1, 0, height)
    edges_in(1, 3, 2, 1)
    settle_edges(1, 1, (1, 3, 2), (0, 2, 2), (1, 2, 1), (1, 1, 0), (0, 1, 1))
    level_in(1, 0)
    gather(1, 0)
    add(1, 0, 0, 0)
    settle(1, 0, 0, height)
    edges_in(1, 0)
    settle_edges(1, 0, (0, 0, 0))

    for frame in (1, 0):
        wait_sent(1, frame)


def shards(sizes, frames_in, weight_first, scale_first, weight_second, scale_second):
    frames, height, width, channels = frames_in.shape
    anywhere = pl.BlockSpec(memory_space=pl.ANY)
    lines = width * channels // 128
    flat = (3, 9 * channels, channels)
    half = jnp.bfloat16
    kinds = kind_counts(sizes)[2]
    return pl.pallas_call(
        functools.partial(kernel, sizes),
        out_shape=pltpu.VMEM(frames_in.shape, half),
        in_specs=[anywhere] * 5,
        out_specs=pl.BlockSpec(memory_space=pltpu.VMEM),
        scratch_shapes=[
            pltpu.VMEM(frames_in.shape, half),
            pltpu.VMEM((2, 1, channels), jnp.float32),
            pltpu.VMEM((2, *flat), half),
            pltpu.VMEM((2, frames, height, lines, 128), half),
            pltpu.VMEM((2, frames, 2, 2 * height, 128), half),
            pltpu.VMEM((2, frames, height, lines, 128), half),
            pltpu.VMEM((2, 2 * frames, 2, lines, 128), half),
            pltpu.VMEM((2, 2 * frames, 3, 2, 2 * height, 128), half),
            pltpu.VMEM((2 * frames, height * width, 9 * channels), half),
            pltpu.VMEM((frames, height * width, channels), jnp.float32),
            pltpu.SemaphoreType.DMA((6,)),
            pltpu.SemaphoreType.DMA((frames * kinds,)),
            pltpu.SemaphoreType.DMA((2, frames * kinds)),
            pltpu.SemaphoreType.REGULAR,
        ],
        compiler_params=pltpu.CompilerParams(collective_id=0, has_side_effects=True),
        name="conv_block",
    )(
        frames_in,
        weight_first.reshape(flat),
        scale_first.reshape(1, channels),
        weight_second.reshape(flat),
        scale_second.reshape(1, channels),
    )


def solution(mesh):
    sizes = tuple(mesh.shape[axis] for axis in AXES)
    return jax.shard_map(
        functools.partial(shards, sizes),
        mesh=mesh,
        in_specs=(P(("groups", "frame"), "strip", "slab", None), P(), P(), P(), P()),
        out_specs=P(("groups", "frame"), "strip", "slab", None),
        check_vma=False,
    )
```
